32 devices in a mesh: chan: 8 (over y, x, core), rec: 4 (over z).
Axes of the slice: x: 2, y: 2, z: 4, core: 2. Of those that a mesh axis runs over, the one named last changes fastest.
Arguments:
- records: bfloat16 [4, 4096, 2048], P('rec', 'chan'), as said below
- fir_choice: int32 [2048], P('chan'), may hold values from 0 to 15
- bank: float32 [16, 64], replicated, may hold values from -4 to 4
- partner: int32 [3, 8], replicated, may hold values from 0 to 7, as said below
Outputs:
- xcorr: float32 [3, 2048, 8, 256], P(None, 'chan', 'rec')
The draws below stay inside these ranges and needn't reach their ends.
Inputs may be any that keep to these rules, and one draw needn't show every extreme that they name: Each round is a pairing by exclusive or: partner[r, a] = a XOR m_r for one mask m_r of 1 to 7 a round, the masks of different rounds differ. `records`: samples are finite and not all zero in any channel of any record.
All inputs are finite; a program needn't handle non-finite values.
Results may differ from the reference program's by a relative error of at most 0.0055.
Values may be sent and summed in bfloat16 or wider, within the bound.
No kernel may reach another device: no remote copies, remote signals or barrier semaphores. Data moves between devices by JAX's collectives and lax.ppermute only.
A program may use at most 128 MiB of HBM per device.

```python
import math
import jax
import jax.numpy as jnp
from jax import lax

BLOCK = 256
TAPS = 64
LAGS = 8
BANKS = 16
ROUNDS = 3
TIME = 4096
NBLK = 8
CHANNELS = 2048
RECORDS = 4


def draw_records(key, part):
    key_scale, key_env, key_base = jax.random.split(key, 3)
    chan_scale = jnp.exp(jax.random.uniform(key_scale, (RECORDS, 1, 1, CHANNELS), jnp.float32, 0.0, math.log(10.0)))
    envelope = jnp.exp(jax.random.uniform(key_env, (RECORDS, TIME // 64, 1, CHANNELS), jnp.float32, math.log(0.3), math.log(3.0)))
    base = jax.random.normal(key_base, (RECORDS, TIME // 64, 64, CHANNELS), jnp.float32)
    values = base * envelope * chan_scale
    return values.reshape(RECORDS, TIME, CHANNELS).astype(jnp.bfloat16)


def draw_partner(key, part):
    masks = (jax.random.permutation(key, NBLK - 1)[:ROUNDS] + 1).astype(jnp.int32)
    blocks = jnp.arange(NBLK, dtype=jnp.int32)
    return jnp.bitwise_xor(blocks[None, :], masks[:, None]).astype(jnp.int32)


def touch_ends(result, own_key, least, top_value):
    index_at = [jax.random.randint(jax.random.fold_in(own_key, axis), (), 0, length) for axis, length in enumerate(result.shape)]
    longest = result.shape.index(max(result.shape))
    beside = index_at[:longest] + [(index_at[longest] + 1) % result.shape[longest]] + index_at[longest + 1:]
    return result.at[tuple(index_at)].set(least).at[tuple(beside)].set(top_value)


def bell_draw(rng, extent, deviation, limit, kind=jnp.bfloat16):
    return jnp.clip(deviation * jax.random.normal(rng, extent, jnp.float32), -limit, limit).astype(kind)


def setup_inputs(seed: int = 0) -> dict:
    splits = jax.random.split(jax.random.key(seed), 5)
    records = draw_records(jax.random.fold_in(splits[4], 71), 0)
    fir_choice = touch_ends(jax.random.randint(splits[1], (CHANNELS,), 0, BANKS), jax.random.fold_in(splits[1], 1), 0, BANKS - 1).astype(jnp.int32)
    bank = bell_draw(splits[2], (BANKS, TAPS), 0.3, 4.0, jnp.float32)
    partner = draw_partner(jax.random.fold_in(splits[4], 71), 0)
    return dict(records=records, fir_choice=fir_choice, bank=bank, partner=partner)


def whiten_one(raw, taps):
    signal = raw.astype(jnp.float32)
    padded = jnp.pad(signal, ((TAPS - 1, 0), (0, 0)))
    total = jnp.zeros(signal.shape, jnp.float32)
    for tap in range(TAPS):
        total = total + taps[:, tap][None, :] * padded[TAPS - 1 - tap:TAPS - 1 - tap + TIME, :]
    whitened = total.astype(jnp.bfloat16)
    values = whitened.astype(jnp.float32)
    power = lax.optimization_barrier(jnp.mean(values * values, axis=0))
    return (values * lax.rsqrt(power + 1e-06)[None, :]).astype(jnp.bfloat16)

def reference(records, fir_choice, bank, partner):
    taps = bank[fir_choice]
    normed = lax.map(lambda raw: whiten_one(raw, taps), records)
    scale = 1.0 / math.sqrt(TIME)
    rounds_out = []
    for step in range(ROUNDS):

        def one_block(block_id):
            start = (block_id * BLOCK).astype(jnp.int32)
            other = (partner[step, block_id] * BLOCK).astype(jnp.int32)
            own = lax.dynamic_slice_in_dim(normed, start, BLOCK, 2)
            mate = lax.dynamic_slice_in_dim(normed, other, BLOCK, 2)
            mate = jnp.pad(mate, ((0, 0), (0, LAGS), (0, 0)))
            total = jnp.zeros((BLOCK, LAGS * BLOCK), jnp.float32)
            for record in range(RECORDS):
                stacked = jnp.concatenate([mate[record, lag:lag + TIME, :] for lag in range(LAGS)], axis=1)
                product = lax.dot_general(own[record], stacked, (((0,), (0,)), ((), ())), preferred_element_type=jnp.float32)
                total = total + product * scale
            return total.reshape(BLOCK, LAGS, BLOCK)
        blocks = lax.map(one_block, jnp.arange(NBLK, dtype=jnp.int32))
        rounds_out.append(blocks.reshape(CHANNELS, LAGS, BLOCK))
    return jnp.stack(rounds_out, axis=0)
```

```python
import functools
import math

import jax
import jax.numpy as jnp
from jax import lax
from jax.experimental import pallas as pl
from jax.experimental.pallas import tpu as pltpu
from jax.sharding import PartitionSpec as P

LAGS = 8
ROUNDS = 3
EXT = 8
HALO = 80
LANES = 128
F32 = jnp.float32
BF16 = jnp.bfloat16


def swap(x, axis, mask):
    return lax.ppermute(x, axis, [(i, i ^ mask) for i in range(lax.axis_size(axis))])


def whiten_kernel(me_ref, x_ref, halo_ref, choice_ref, bank_ref, w_ref, p_ref, xe, tp, ws):
    taps = bank_ref.shape[1]
    span = x_ref.shape[0]
    xe[0:HALO, :] = halo_ref[...].astype(F32)
    xe[HALO : HALO + span, :] = x_ref[...].astype(F32)
    choice = choice_ref[0]
    for group in range(taps // 8):
        table = jnp.zeros((8, LANES), F32)
        for entry in range(bank_ref.shape[0]):
            table = jnp.where(choice == entry, bank_ref[entry, 8 * group : 8 * group + 8, :], table)
        for sub in range(8):
            tp[8 * group + sub] = jnp.broadcast_to(table[sub : sub + 1, :], (8, LANES))
    tiles = (EXT + span) // 8
    per = 13
    first = HALO - EXT

    def group_body(g, carry):
        base = pl.multiple_of(g * (per * 8), 8)
        acc = [jnp.zeros((8, LANES), F32) for _ in range(per)]
        for sub in range(8):
            coef = [tp[8 * q + sub] for q in range(taps // 8)]
            for v in range(1 - taps // 8, per):
                tile = xe[pl.ds(base + (first + 8 * v - sub), 8), :]
                for q in range(taps // 8):
                    if 0 <= v + q < per:
                        acc[v + q] = acc[v + q] + coef[q] * tile
        for i in range(per):
            ws[pl.ds(base + 8 * i, 8), :] = acc[i]
        return carry

    lax.fori_loop(0, tiles // per, group_body, 0)
    rounded = ws[...].astype(BF16)
    w_ref[...] = rounded
    own = rounded.astype(F32)[EXT:, :]
    p_ref[0] = jnp.sum((own * own).reshape(span // 8, 8, LANES), axis=0)


def whiten(me, x, halo, choice, bank, half):
    span, channels = x.shape
    blocks = choice.shape[0]
    return pl.pallas_call(
        whiten_kernel,
        out_shape=(
            jax.ShapeDtypeStruct((EXT + span, blocks * LANES), BF16),
            jax.ShapeDtypeStruct((blocks, 8, LANES), F32),
        ),
        grid_spec=pltpu.PrefetchScalarGridSpec(
            num_scalar_prefetch=1,
            grid=(blocks,),
            in_specs=[
                pl.BlockSpec((span, LANES), lambda b, m: (0, 2 * b + half)),
                pl.BlockSpec((HALO, LANES), lambda b, m: (0, 2 * b + half)),
                pl.BlockSpec((1, 1, LANES), lambda b, m: (jnp.bitwise_xor(b, m[0]), 0, half)),
                pl.BlockSpec(bank.shape, lambda b, m: (0, 0, 0)),
            ],
            out_specs=[
                pl.BlockSpec((EXT + span, LANES), lambda b, m: (0, b)),
                pl.BlockSpec((1, 8, LANES), lambda b, m: (b, 0, 0)),
            ],
            scratch_shapes=[
                pltpu.VMEM((HALO + span, LANES), F32),
                pltpu.VMEM((bank.shape[1], 8, LANES), F32),
                pltpu.VMEM((EXT + span, LANES), F32),
            ],
        ),
        cost_estimate=pl.CostEstimate(flops=10**10, bytes_accessed=3 * 2**20, transcendentals=0),
        name=f"whiten{half}",
    )(me, x, halo, choice, bank)


def correlate_kernel(spans, carried, last, *refs):
    ids, scale_ref = refs[0], refs[1]
    pieces = refs[2 : 2 + 2 * spans]
    at = 2 + 2 * spans
    if carried:
        acc_in = refs[at]
        at += 1
    outs = refs[at : at + (2 * ROUNDS if last else 1)]
    at += len(outs)
    a_buf, b_buf, a_norm, a_shift, b_turn, acc, sem = refs[at:]
    length = b_buf.shape[2]
    width = 2 * LANES

    def copies(k):
        for role in range(1 + ROUNDS):
            for half in range(2):
                column = pl.ds(pl.multiple_of(ids[role] * LANES, LANES), LANES)
                lanes = pl.ds(half * LANES, LANES)
                source = pieces[2 * k + half]
                if role == 0:
                    yield pltpu.make_async_copy(
                        source.at[:, column], a_buf.at[k, :, lanes], sem.at[k, role, half]
                    )
                else:
                    yield pltpu.make_async_copy(
                        source.at[pl.ds(EXT, length), column],
                        b_buf.at[k, role - 1, :, lanes],
                        sem.at[k, role, half],
                    )

    for k in range(spans):
        for copy in copies(k):
            copy.start()

    for k in range(spans):
        for copy in copies(k):
            copy.wait()
        a_norm[...] = a_buf[k].astype(F32) * scale_ref[ids[0]]
        for lag in range(LAGS):
            place = pl.multiple_of(ids[1 + ROUNDS + lag] * width, width)
            shifted = a_norm[EXT - lag : EXT - lag + length, :]
            a_shift[:, pl.ds(place, width)] = shifted.astype(BF16)
        for r in range(ROUNDS):
            scaled = (b_buf[k, r].astype(F32) * scale_ref[ids[1 + r]]).astype(BF16)
            b_turn[r * width : (r + 1) * width, :] = scaled.T

        def column_body(c, carry, k=k):
            column = pl.ds(pl.multiple_of(c * width, width), width)
            product = jnp.dot(b_turn[...], a_shift[:, column], preferred_element_type=F32)
            if k > 0:
                product = product + acc[:, column]
            elif carried:
                product = product + acc_in[:, column]
            acc[:, column] = product
            return carry

        lax.fori_loop(0, LAGS, column_body, 0)

    if last:
        unit = 1.0 / math.sqrt(8 * length)
        part = LAGS // 2 * width
        for r in range(ROUNDS):
            rows = slice(r * width, (r + 1) * width)
            outs[r][...] = (acc[rows, 0:part] * unit).astype(BF16)
            outs[ROUNDS + r][...] = acc[rows, part : 2 * part] * unit
    else:
        outs[0][...] = acc[...]


def correlate(ids, scale, pieces, carried, last):
    spans = len(pieces) // 2
    rows = pieces[0].shape[0]
    length = rows - EXT
    width = 2 * LANES
    whole = (ROUNDS * width, LAGS * width)
    part = (width, LAGS // 2 * width)
    vmem = pl.BlockSpec(memory_space=pltpu.VMEM)
    anywhere = pl.BlockSpec(memory_space=pl.ANY)
    if last:
        shapes = [jax.ShapeDtypeStruct(part, BF16)] * ROUNDS + [
            jax.ShapeDtypeStruct(part, F32)
        ] * ROUNDS
    else:
        shapes = [jax.ShapeDtypeStruct(whole, F32)]
    extra = [] if carried is None else [carried]
    flops = 2 * spans * length * whole[0] * whole[1]
    return pl.pallas_call(
        functools.partial(correlate_kernel, spans, carried is not None, last),
        out_shape=shapes,
        in_specs=[pl.BlockSpec(memory_space=pltpu.SMEM), vmem]
        + [anywhere] * (2 * spans)
        + [vmem] * len(extra),
        out_specs=[vmem] * len(shapes),
        scratch_shapes=[
            pltpu.VMEM((spans, rows, width), BF16),
            pltpu.VMEM((spans, ROUNDS, length, width), BF16),
            pltpu.VMEM((rows, width), F32),
            pltpu.VMEM((length, LAGS * width), BF16),
            pltpu.VMEM((ROUNDS * width, length), BF16),
            pltpu.VMEM(whole, F32),
            pltpu.SemaphoreType.DMA((spans, 1 + ROUNDS, 2)),
        ],
        cost_estimate=pl.CostEstimate(flops=flops, bytes_accessed=spans * 2**20, transcendentals=0),
        name="correlate_last" if last else "correlate_first",
    )(ids, scale, *pieces, *extra)


def finish_kernel(*refs):
    out = refs[-1]
    width = out.shape[1]
    for r in range(ROUNDS):
        total = refs[r][...] + refs[ROUNDS + r][...].astype(F32)
        for p in range(out.shape[2]):
            out[r, :, p, :] = total[:, p * width : (p + 1) * width].T


def finish(kept, received):
    width = 2 * LANES
    lags = kept[0].shape[1] // width
    return pl.pallas_call(
        finish_kernel,
        out_shape=jax.ShapeDtypeStruct((ROUNDS, width, lags, width), F32),
        in_specs=[pl.BlockSpec(memory_space=pltpu.VMEM)] * (2 * ROUNDS),
        out_specs=pl.BlockSpec(memory_space=pltpu.VMEM),
        cost_estimate=pl.CostEstimate(flops=10**6, bytes_accessed=4 * 2**20, transcendentals=0),
        name="finish",
    )(*kept, *received)


def per_device_cube(records, fir_choice, bank, partner):
    x = records[0]
    span = x.shape[0]
    blocks = lax.axis_size("chan")
    me = lax.axis_index("chan")
    z = lax.axis_index("rec")
    halo = lax.ppermute(x[span - HALO :, :], "chan", [(i, i + 1) for i in range(blocks - 1)])
    choice = fir_choice[None, None, :]
    for level in range(3):
        choice = jnp.concatenate([choice, swap(choice, "chan", 1 << level)], axis=0)
    wide = jnp.broadcast_to(bank[:, :, None], bank.shape + (LANES,))
    me1 = me.astype(jnp.int32)[None]
    w, power = [], []
    for half in range(2):
        piece, squares = whiten(me1, x, halo, choice, wide, half)
        w.append(piece)
        power.append(jnp.sum(squares, axis=1))
    beside_x = [swap(w[h], "chan", 2) for h in range(2)]
    beside_y = [swap(w[h], "chan", 4) for h in range(2)]
    across = [swap(beside_y[0], "chan", 2), swap(beside_x[1], "chan", 4)]
    total = jnp.concatenate(power, axis=1)
    for level in range(3):
        total = total + swap(total, "chan", 1 << level)
    scale = lax.rsqrt(total * (1.0 / (blocks * span)) + 1e-06)[:, None, :]

    zl, zh = jnp.bitwise_and(z, 1), jnp.right_shift(z, 1)
    places = []
    for lag in range(LAGS):
        keep = (((lag >> 1) & 1) == zl).astype(jnp.int32)
        mine = ((lag >> 2) == zh).astype(jnp.int32)
        places.append(keep * 4 + mine * 2 + (lag & 1))
    mates = [lax.dynamic_index_in_dim(partner[r], me, keepdims=False) for r in range(ROUNDS)]
    ids = jnp.stack([me.astype(jnp.int32)] + mates + places)

    early = w + beside_x + beside_y
    other = [swap(piece, "chan", 1) for piece in early]
    across_other = [swap(piece, "chan", 1) for piece in across]
    held = correlate(ids, scale, early + other, None, False)[0]
    ready = correlate(ids, scale, across + across_other, held, True)
    kept, received = [], []
    half_width = ready[0].shape[1] // 2
    for r in range(ROUNDS):
        summed = ready[ROUNDS + r] + swap(ready[r], "rec", 1).astype(F32)
        received.append(swap(summed[:, :half_width].astype(BF16), "rec", 2))
        kept.append(summed[:, half_width:])
    return finish(kept, received)


def partner_2(x, axis, apart):
    return lax.ppermute(x, axis, [(i, i ^ 1 << apart) for i in range(lax.axis_size(axis))])


def whiten_block(raw, taps):
    length = raw.shape[0]
    width = taps.shape[1]
    signal = raw.astype(jnp.float32)
    padded = jnp.pad(signal, ((width - 1, 0), (0, 0)))
    total = jnp.zeros(signal.shape, jnp.float32)
    for tap in range(width):
        total = (
            total + taps[:, tap][None, :] * padded[width - 1 - tap : width - 1 - tap + length, :]
        )
    whitened = total.astype(jnp.bfloat16)
    values = whitened.astype(jnp.float32)
    power = jnp.mean(values * values, axis=0)
    return (values * lax.rsqrt(power + 1e-06)[None, :]).astype(jnp.bfloat16)


def lagged_term(own, mate):
    length = own.shape[0]
    padded = jnp.pad(mate, ((0, LAGS), (0, 0)))
    stacked = jnp.concatenate([padded[lag : lag + length, :] for lag in range(LAGS)], axis=1)
    product = lax.dot_general(
        own, stacked, (((0,), (0,)), ((), ())), preferred_element_type=jnp.float32
    )
    return (product * (1.0 / math.sqrt(length))).reshape(own.shape[1], LAGS, own.shape[1])


def per_device(records, fir_choice, bank, partner):
    blocks_all = lax.axis_size("chan")
    width = records.shape[2] // blocks_all
    span = records.shape[1]
    local = records[0].reshape(span, blocks_all, width)
    owned = lax.all_to_all(local, "chan", split_axis=1, concat_axis=0, tiled=True)[:, 0, :]
    onehot = (fir_choice[:, None] == jnp.arange(bank.shape[0], dtype=jnp.int32)[None, :]).astype(
        jnp.float32
    )
    taps = jnp.dot(
        onehot, bank, precision=lax.Precision.HIGHEST, preferred_element_type=jnp.float32
    )
    normed = whiten_block(owned, taps)
    terms = []
    levels = blocks_all.bit_length() - 1
    for step in range(ROUNDS):
        mask = partner[step, 0]
        moving = normed
        for level in range(levels):
            flag = jnp.bitwise_and(jnp.right_shift(mask, level), 1) == 1
            swapped = partner_2(moving, "chan", level)
            moving = jnp.where(flag, swapped, moving)
        terms.append(lagged_term(normed, moving))
    summed = [lax.psum_scatter(term, "rec", scatter_dimension=1, tiled=True) for term in terms]
    return jnp.stack(summed, axis=0)


def solution(mesh):
    placed = (P("rec", "chan", None), P("chan"), P(), P())
    cube = mesh.shape["chan"] == 8 and mesh.shape["rec"] == 4
    return jax.shard_map(
        per_device_cube if cube else per_device,
        mesh=mesh,
        in_specs=placed,
        out_specs=P(None, "chan", "rec", None),
        check_vma=False,
    )
```

```python
import functools
import math

import jax
import jax.numpy as jnp
from jax import lax
from jax.experimental import pallas as pl
from jax.experimental.pallas import tpu as pltpu
from jax.sharding import PartitionSpec as P


LAGS = 8
ROUNDS = 3
EXT = 8
HALO = 80
LANES = 128
F32 = jnp.float32
BF16 = jnp.bfloat16


def swap(x, axis, mask):
    return lax.ppermute(x, axis, [(i, i ^ mask) for i in range(lax.axis_size(axis))])


def whiten_kernel(start, me_ref, x_ref, halo_ref, c0, c1, c2, c3, bank_ref, w_ref, p_ref, xe, tp, ws):
    taps = bank_ref.shape[1]
    span = x_ref.shape[0]
    xe[0:HALO, :] = halo_ref[...].astype(F32)
    xe[HALO : HALO + span, :] = x_ref[...].astype(F32)
    mask = jnp.bitwise_xor(pl.program_id(0) + start, me_ref[0])
    row, which = jnp.bitwise_and(mask, 1), jnp.right_shift(mask, 1)
    choice = c0[row]
    for index, other in ((1, c1), (2, c2), (3, c3)):
        choice = jnp.where(which == index, other[row], choice)
    for group in range(taps // 8):
        table = jnp.zeros((8, LANES), F32)
        for entry in range(bank_ref.shape[0]):
            table = jnp.where(choice == entry, bank_ref[entry, 8 * group : 8 * group + 8, :], table)
        for sub in range(8):
            tp[8 * group + sub] = jnp.broadcast_to(table[sub : sub + 1, :], (8, LANES))
    tiles = (EXT + span) // 8
    per = 13
    first = HALO - EXT

    def group_body(g, carry):
        base = pl.multiple_of(g * (per * 8), 8)
        acc = [jnp.zeros((8, LANES), F32) for _ in range(per)]
        for sub in range(8):
            coef = [tp[8 * q + sub] for q in range(taps // 8)]
            for v in range(1 - taps // 8, per):
                tile = xe[pl.ds(base + (first + 8 * v - sub), 8), :]
                for q in range(taps // 8):
                    if 0 <= v + q < per:
                        acc[v + q] = acc[v + q] + coef[q] * tile
        for i in range(per):
            ws[pl.ds(base + 8 * i, 8), :] = acc[i]
        return carry

    lax.fori_loop(0, tiles // per, group_body, 0)
    rounded = ws[...].astype(BF16)
    w_ref[...] = rounded
    own = rounded.astype(F32)[EXT:, :]
    p_ref[0] = jnp.sum(own * own, axis=0, keepdims=True)


def whiten(me, x, halo, choices, bank, half, quad):
    span = x.shape[0]
    blocks = len(choices)
    start = quad * blocks
    lane = lambda b, m: (0, 2 * (b + start) + half)
    return pl.pallas_call(
        functools.partial(whiten_kernel, start),
        out_shape=(
            jax.ShapeDtypeStruct((EXT + span, blocks * LANES), BF16),
            jax.ShapeDtypeStruct((blocks, 1, LANES), F32),
        ),
        grid_spec=pltpu.PrefetchScalarGridSpec(
            num_scalar_prefetch=1,
            grid=(blocks,),
            in_specs=[
                pl.BlockSpec((span, LANES), lane),
                pl.BlockSpec((HALO, LANES), lane),
                *[pl.BlockSpec((2, 1, LANES), lambda b, m: (0, 0, half))] * blocks,
                pl.BlockSpec(bank.shape, lambda b, m: (0, 0, 0)),
            ],
            out_specs=[
                pl.BlockSpec((EXT + span, LANES), lambda b, m: (0, b)),
                pl.BlockSpec((1, 1, LANES), lambda b, m: (b, 0, 0)),
            ],
            scratch_shapes=[
                pltpu.VMEM((HALO + span, LANES), F32),
                pltpu.VMEM((bank.shape[1], 8, LANES), F32),
                pltpu.VMEM((EXT + span, LANES), F32),
            ],
        ),
        compiler_params=pltpu.CompilerParams(vmem_limit_bytes=12 * 2**20),
        cost_estimate=pl.CostEstimate(flops=5 * 10**9, bytes_accessed=2**20, transcendentals=0),
    )(me, x, halo, *choices, bank)


def correlate_kernel(spans, halves, carried, last, *refs):
    ids = refs[0]
    scales = refs[1 : 1 + halves]
    at = 1 + halves
    pieces = refs[at : at + 2 * halves * spans]
    at += 2 * halves * spans
    jobs = 1 if halves == 1 else 2
    acc_in = refs[at : at + jobs] if carried else None
    at += jobs if carried else 0
    chunks = 1 if halves == 1 else 3
    outs = refs[at : at + ((3 if chunks == 1 else 10) if last else jobs)]
    at += len(outs)
    a_buf, b_buf, a_norm, shift0, shift1, turn0, turn1, sem = refs[at : at + 8]
    accs = refs[at + 8 : at + 8 + jobs] if last else outs
    a_shift, b_turn = (shift0, shift1), (turn0, turn1)
    length = b_buf.shape[3]
    third = ROUNDS * LANES
    roles = 1 + ROUNDS
    pairs = spans // 2

    def copy(k, h, role, quad):
        column = pl.ds(pl.multiple_of(ids[roles + role] * LANES, LANES), LANES)
        source = pieces[(k * halves + h) * 2 + quad]
        if role == 0:
            return pltpu.make_async_copy(source.at[:, column], a_buf.at[k, h], sem.at[k, h, role])
        return pltpu.make_async_copy(
            source.at[pl.ds(EXT, length), column], b_buf.at[k, h, role - 1], sem.at[k, h, role]
        )

    for k in range(spans):
        for h in range(halves):
            for role in range(roles):
                upper = ids[role] >= 4

                @pl.when(upper)
                def _(k=k, h=h, role=role):
                    copy(k, h, role, 1).start()

                @pl.when(jnp.logical_not(upper))
                def _(k=k, h=h, role=role):
                    copy(k, h, role, 0).start()

    own_scale = [scales[h][ids[0]] for h in range(halves)]
    mate_scale = [[scales[h][ids[1 + r]] for r in range(ROUNDS)] for h in range(halves)]
    place = [
        pl.multiple_of(ids[2 * roles + lag] * LANES, LANES) for lag in range(LAGS)
    ]

    def arrive(pair):
        for k in (2 * pair, 2 * pair + 1):
            for h in range(halves):
                for role in range(roles):
                    copy(k, h, role, 0).wait()

    def prepare(pair):
        steps = []
        for j in range(2):
            k = 2 * pair + j
            rows = slice(j * length, (j + 1) * length)
            for h in range(halves):

                def normalize(k=k, j=j, h=h):
                    a_norm[j, h] = a_buf[k, h].astype(F32) * own_scale[h]

                steps.append(normalize)
                for lag in range(LAGS):

                    def shift(j=j, h=h, rows=rows, lag=lag):
                        moved = a_norm[j, h, EXT - lag : EXT - lag + length, :]
                        a_shift[pair % 2][h, rows, pl.ds(place[lag], LANES)] = moved.astype(BF16)

                    steps.append(shift)
                for r in range(ROUNDS):

                    def turn(k=k, h=h, rows=rows, r=r):
                        scaled = (b_buf[k, h, r].astype(F32) * mate_scale[h][r]).astype(BF16)
                        top = h * third + r * LANES
                        b_turn[pair % 2][top : top + LANES, rows] = scaled.T

                    steps.append(turn)
        return steps

    def contract(pair, job, c):
        low = third if halves == 2 and job == 0 else 0
        column = slice(c * 2 * LANES, (c + 1) * 2 * LANES)
        product = jnp.dot(
            b_turn[pair % 2][low:, :],
            a_shift[pair % 2][job, :, column],
            preferred_element_type=F32,
        )
        if pair > 0:
            product = product + accs[job][:, column]
        elif carried:
            product = product + acc_in[job][:, column]
        if pair < pairs - 1 or not last:
            accs[job][:, column] = product
            return
        product = product * (1.0 / math.sqrt(8 * length))
        for part in range(product.shape[0] // third):
            value = product[part * third : (part + 1) * third, :]
            chunk = job + part
            if chunk == 2:
                outs[6 + c][...] = value.astype(outs[6 + c].dtype)
            elif c < 2:
                outs[3 * chunk][:, column] = value.astype(BF16)
            else:
                outs[3 * chunk + c - 1][...] = value

    arrive(0)
    for step in prepare(0):
        step()
    for pair in range(pairs):
        steps = []
        if pair + 1 < pairs:
            arrive(pair + 1)
            steps = prepare(pair + 1)
        turns = [(job, c) for job in range(jobs) for c in range(LAGS // 2)]
        each = -(-len(steps) // len(turns))
        for at_turn, (job, c) in enumerate(turns):
            contract(pair, job, c)
            for step in steps[at_turn * each : (at_turn + 1) * each]:
                step()


def correlate(ids, scales, pieces, carried, last):
    spans, halves = len(pieces), len(pieces[0])
    rows = pieces[0][0][0].shape[0]
    length = rows - EXT
    third = ROUNDS * LANES
    wide = LAGS * LANES
    sizes = [third] if halves == 1 else [third, 2 * third]
    chunks = 1 if halves == 1 else 3
    vmem = pl.BlockSpec(memory_space=pltpu.VMEM)
    anywhere = pl.BlockSpec(memory_space=pl.ANY)
    if last:
        shapes = [
            jax.ShapeDtypeStruct((third, 4 * LANES), BF16),
            jax.ShapeDtypeStruct((third, 2 * LANES), F32),
            jax.ShapeDtypeStruct((third, 2 * LANES), F32),
        ] * min(chunks, 2)
        if chunks == 3:
            shapes += [jax.ShapeDtypeStruct((third, 2 * LANES), BF16)] * 3
            shapes += [jax.ShapeDtypeStruct((third, 2 * LANES), F32)]
    else:
        shapes = [jax.ShapeDtypeStruct((size, wide), F32) for size in sizes]
    flat = [pieces[k][h][q] for k in range(spans) for h in range(halves) for q in range(2)]
    flops = 2 * spans * length * sum(sizes) * wide
    return pl.pallas_call(
        functools.partial(correlate_kernel, spans, halves, carried is not None, last),
        out_shape=shapes,
        in_specs=[pl.BlockSpec(memory_space=pltpu.SMEM)]
        + [vmem] * halves
        + [anywhere] * len(flat)
        + [vmem] * len(carried or []),
        out_specs=[vmem] * len(shapes),
        scratch_shapes=[
            pltpu.VMEM((spans, halves, rows, LANES), BF16),
            pltpu.VMEM((spans, halves, ROUNDS, length, LANES), BF16),
            pltpu.VMEM((2, halves, rows, LANES), F32),
            pltpu.VMEM((halves, 2 * length, wide), BF16),
            pltpu.VMEM((halves, 2 * length, wide) if spans > 2 else (8, LANES), BF16),
            pltpu.VMEM((halves * third, 2 * length), BF16),
            pltpu.VMEM((halves * third, 2 * length) if spans > 2 else (8, LANES), BF16),
            pltpu.SemaphoreType.DMA((spans, halves, 1 + ROUNDS)),
        ]
        + ([pltpu.VMEM((size, wide), F32) for size in sizes] if last else []),
        compiler_params=pltpu.CompilerParams(vmem_limit_bytes=30 * 2**20),
        cost_estimate=pl.CostEstimate(
            flops=2 * flops, bytes_accessed=spans * 2**19, transcendentals=0
        ),
    )(ids, *scales, *flat, *(carried or []))


def finish_kernel(*refs):
    out = refs[-1]
    at = 0
    for chunk in range(4):
        hi, hj = chunk >> 1, chunk & 1
        count = 4 if chunk == 3 else 3
        total = refs[at][...]
        for other in refs[at + 1 : at + count]:
            total = total + other[:, other.shape[1] - 2 * LANES :].astype(F32)
        at += count
        for r in range(ROUNDS):
            for p in range(out.shape[2]):
                tile = total[r * LANES : (r + 1) * LANES, p * LANES : (p + 1) * LANES]
                out[r, hi * LANES : (hi + 1) * LANES, p, hj * LANES : (hj + 1) * LANES] = tile.T


def finish(parts):
    flat = [value for part in parts for value in part]
    return pl.pallas_call(
        finish_kernel,
        out_shape=jax.ShapeDtypeStruct((ROUNDS, 2 * LANES, 2, 2 * LANES), F32),
        in_specs=[pl.BlockSpec(memory_space=pltpu.VMEM)] * len(flat),
        out_specs=pl.BlockSpec(memory_space=pltpu.VMEM),
        compiler_params=pltpu.CompilerParams(vmem_limit_bytes=12 * 2**20),
        cost_estimate=pl.CostEstimate(flops=10**6, bytes_accessed=4 * 2**20, transcendentals=0),
        name="finish",
    )(*flat)


def per_device_cube(records, fir_choice, bank, partner):
    return cube_body(records, fir_choice, bank, partner)


def cube_body(records, fir_choice, bank, partner):
    x = records[0]
    span = x.shape[0]
    blocks = lax.axis_size("chan")
    me = lax.axis_index("chan").astype(jnp.int32)
    z = lax.axis_index("rec")
    choice = fir_choice[None, None, :]
    wide = jnp.broadcast_to(bank[:, :, None], bank.shape + (LANES,))
    beside = swap(choice, "chan", 1)
    beside, wide = lax.optimization_barrier((beside, wide))
    choice = jnp.concatenate([choice, beside], axis=0)
    halo = lax.ppermute(x[span - HALO :, :], "chan", [(i, i + 1) for i in range(blocks - 1)])
    choices = [choice] + [swap(choice, "chan", m) for m in (2, 4, 6)]

    zl, zh = jnp.bitwise_and(z, 1), jnp.right_shift(z, 1)
    places = []
    for lag in range(LAGS):
        keep = (((lag >> 1) & 1) == zl).astype(jnp.int32)
        mine = ((lag >> 2) == zh).astype(jnp.int32)
        places.append(keep * 4 + mine * 2 + (lag & 1))
    mates = lax.dynamic_index_in_dim(partner, me, axis=1, keepdims=False)
    roles = jnp.concatenate([me[None], mates])
    ids = jnp.concatenate([roles, jnp.bitwise_and(roles, 3), jnp.stack(places)])

    own, beside_x, beside_y, across = {}, {}, {}, {}
    scales = []
    for h in range(2):
        power = []
        for q in range(2):
            own[h, q], squares = whiten(me[None], x, halo, choices, wide, h, q)
            power.append(squares)
            beside_x[h, q] = swap(own[h, q], "chan", 2)
            beside_y[h, q] = swap(own[h, q], "chan", 4)
        total = jnp.concatenate(power, axis=0)
        total = total + swap(total, "chan", 1)
        others = [swap(total, "chan", m) for m in (2, 4, 6)]
        total = total + others[0] + (others[1] + others[2])
        scales.append(lax.rsqrt(total * (1.0 / (blocks * span)) + 1e-06))
        across[h, 0] = swap(beside_y[h, 0], "chan", 2)
        across[h, 1] = swap(beside_x[h, 1], "chan", 4)

    def both(piece, h):
        mine = [piece[h, q] for q in range(2)]
        return mine, [swap(mine[q], "chan", 1) for q in range(2)]

    groups = [own, beside_x, beside_y, across]
    spans = []
    for h in range(2):
        spans.append([s for piece in groups for s in both(piece, h)])

    def exchange(send, far, near):
        first = swap(send, "rec", 1)
        handed = (far + first[:, : 2 * LANES].astype(F32)).astype(BF16)
        return near, first, swap(handed, "rec", 2)

    early = correlate(ids, scales[:1], [[s] for s in spans[0]], None, True)
    parts = [exchange(*early)]
    late = [[spans[0][k], spans[1][k]] for k in range(8)]
    held = correlate(ids, scales, late[:6], None, False)
    rest = correlate(ids, scales, late[6:], held, True)
    direct = [swap(rest[6 + c], "rec", m) for c, m in ((1, 1), (0, 3), (2, 2))]
    parts.append(exchange(*rest[0:3]))
    parts.append(exchange(*rest[3:6]))
    parts.append((rest[9], *direct))
    return finish(parts)


def partner_2(x, axis, apart):
    return lax.ppermute(x, axis, [(i, i ^ 1 << apart) for i in range(lax.axis_size(axis))])


def whiten_block(raw, taps):
    length = raw.shape[0]
    width = taps.shape[1]
    signal = raw.astype(jnp.float32)
    padded = jnp.pad(signal, ((width - 1, 0), (0, 0)))
    total = jnp.zeros(signal.shape, jnp.float32)
    for tap in range(width):
        total = (
            total + taps[:, tap][None, :] * padded[width - 1 - tap : width - 1 - tap + length, :]
        )
    whitened = total.astype(jnp.bfloat16)
    values = whitened.astype(jnp.float32)
    power = jnp.mean(values * values, axis=0)
    return (values * lax.rsqrt(power + 1e-06)[None, :]).astype(jnp.bfloat16)


def lagged_term(own, mate):
    length = own.shape[0]
    padded = jnp.pad(mate, ((0, LAGS), (0, 0)))
    stacked = jnp.concatenate([padded[lag : lag + length, :] for lag in range(LAGS)], axis=1)
    product = lax.dot_general(
        own, stacked, (((0,), (0,)), ((), ())), preferred_element_type=jnp.float32
    )
    return (product * (1.0 / math.sqrt(length))).reshape(own.shape[1], LAGS, own.shape[1])


def per_device(records, fir_choice, bank, partner):
    blocks_all = lax.axis_size("chan")
    width = records.shape[2] // blocks_all
    span = records.shape[1]
    local = records[0].reshape(span, blocks_all, width)
    owned = lax.all_to_all(local, "chan", split_axis=1, concat_axis=0, tiled=True)[:, 0, :]
    onehot = (fir_choice[:, None] == jnp.arange(bank.shape[0], dtype=jnp.int32)[None, :]).astype(
        jnp.float32
    )
    taps = jnp.dot(
        onehot, bank, precision=lax.Precision.HIGHEST, preferred_element_type=jnp.float32
    )
    normed = whiten_block(owned, taps)
    terms = []
    levels = blocks_all.bit_length() - 1
    for step in range(ROUNDS):
        mask = partner[step, 0]
        moving = normed
        for level in range(levels):
            flag = jnp.bitwise_and(jnp.right_shift(mask, level), 1) == 1
            swapped = partner_2(moving, "chan", level)
            moving = jnp.where(flag, swapped, moving)
        terms.append(lagged_term(normed, moving))
    summed = [lax.psum_scatter(term, "rec", scatter_dimension=1, tiled=True) for term in terms]
    return jnp.stack(summed, axis=0)


def solution(mesh):
    placed = (P("rec", "chan", None), P("chan"), P(), P())
    cube = mesh.shape["chan"] == 8 and mesh.shape["rec"] == 4
    return jax.shard_map(
        per_device_cube if cube else per_device,
        mesh=mesh,
        in_specs=placed,
        out_specs=P(None, "chan", "rec", None),
        check_vma=False,
    )
```
